32 devices in a mesh: gx: 4 (over y, core), gy: 8 (over z, x).
Axes of the slice: x: 2, y: 2, z: 4, core: 2. Of those that a mesh axis runs over, the one named last changes fastest.
Arguments:
- offsets: float32 [2, 8, 64, 128], P(None, 'gx', 'gy'), may hold values from 0 to 1
- masses: float32 [8, 64, 128], P('gx', 'gy'), may hold values from 0.01 to 0.04
- counts: int32 [8, 64], P('gx', 'gy'), may hold values from 1 to 128, as said below
- source: float32 [8, 64, 128], P('gx', 'gy'), may hold values from -6 to 6
Outputs:
- density: float32 [8, 64, 128], P('gx', 'gy')
- pressure: float32 [8, 64, 128], P('gx', 'gy')
- residual: float32 [8, 64, 128], P('gx', 'gy')
- peaks: float32 [5], replicated
The draws below stay inside these ranges and needn't reach their ends.
Inputs may be any that keep to these rules, and one draw needn't show every extreme that they name: `counts`: each cell's occupied slots come first; some cell holds 128 particles.
All inputs are finite; a program needn't handle non-finite values.
Results may differ from the reference program's by a relative error of at most 0.0003.
Values sent between devices are 32-bit elements; how exact they have to be, the bound alone decides.
No kernel may reach another device: no remote copies, remote signals or barrier semaphores. Data moves between devices by JAX's collectives and lax.ppermute only.
A program may use at most 64 MiB of HBM per device.

```python
import math
import jax
import jax.numpy as jnp
from jax import lax

SLOT = 128
ITERS = 5
NX = 8
NY = 64


def draw_counts(key, part):
    coarse_key = jax.random.fold_in(key, 11)
    fine_key = jax.random.fold_in(key, 12)
    region_rows = (NX + 3) // 4
    region_cols = (NY + 3) // 4
    floor_count = jax.random.randint(coarse_key, (region_rows, region_cols), 1, SLOT + 1)
    floor_count = jnp.repeat(jnp.repeat(floor_count, 4, axis=0), 4, axis=1)[:NX, :NY]
    counts = jax.random.randint(fine_key, (NX, NY), floor_count, SLOT + 1)
    return counts.at[0, 0].set(SLOT).astype(jnp.int32)


def draw_source(key, part):
    rough = jnp.clip(jax.random.normal(jax.random.fold_in(key, 21), (NX, NY, SLOT), jnp.float32), -6.0, 6.0)
    return rough


def level_of(key, dims, cuts, least, top_value):
    def one(dim, parts):
        steps = jax.random.uniform(jax.random.fold_in(jax.random.fold_in(key, 6), dim), (parts,), jnp.float32, least / len(cuts), top_value / len(cuts))
        return jnp.repeat(jnp.exp(steps), dims[dim] // parts).reshape((-1,) + (1,) * (len(dims) - dim - 1))

    level = one(*cuts[0])
    for cut in cuts[1:]:
        level = level * one(*cut)
    return level


def setup_inputs(seed: int = 0) -> dict:
    key_list = jax.random.split(jax.random.key(seed), 5)
    return {
        "offsets": jnp.clip(1.0 * jax.random.uniform(key_list[0], (2, NX, NY, SLOT), jnp.float32) ** level_of(key_list[0], (2, NX, NY, SLOT), ((1, 4), (2, 8)), -0.2, 0.2), 0.0, 1.0),
        "masses": jnp.clip(jnp.exp(math.log(0.04) - 1.3862944 * jax.random.uniform(key_list[1], (NX, NY, SLOT), jnp.float32) ** level_of(key_list[1], (NX, NY, SLOT), ((0, 4), (1, 8)), -0.2, 0.2)), 0.01, 0.04),
        "counts": draw_counts(jax.random.fold_in(key_list[4], 71), 0),
        "source": draw_source(jax.random.fold_in(key_list[4], 71), 0),
    }


BASE_STIFF = 0.5
PAIR_SCALE = 0.05
NEIGHBOUR_STEPS = [(step_x, step_y) for step_x in (-1, 0, 1) for step_y in (-1, 0, 1)]


def near_view(padded, step_x, step_y):
    row_count = padded.shape[-3] - 2
    col_count = padded.shape[-2] - 2
    return padded[..., 1 + step_x:1 + step_x + row_count, 1 + step_y:1 + step_y + col_count, :]


def kernel_terms(own_cells, nearby, step_x, step_y):
    offset_x = (step_x + nearby[0][..., None, :]) - own_cells[0][..., :, None]
    offset_y = (step_y + nearby[1][..., None, :]) - own_cells[1][..., :, None]
    return jnp.maximum(1.0 - (offset_x * offset_x + offset_y * offset_y), 0.0)


def density_block(padded):
    own_cells = near_view(padded, 0, 0)
    summed = jnp.zeros(own_cells.shape[1:], jnp.float32)
    for step_x, step_y in NEIGHBOUR_STEPS:
        nearby = near_view(padded, step_x, step_y)
        falloff = kernel_terms(own_cells, nearby, step_x, step_y)
        summed = summed + jnp.sum(falloff * falloff * falloff * nearby[2][..., None, :], axis=-1)
    return 1.0 + summed


def pair_weights(padded, step_x, step_y):
    own_cells = near_view(padded, 0, 0)
    nearby = near_view(padded, step_x, step_y)
    falloff = kernel_terms(own_cells, nearby, step_x, step_y)
    pairing = own_cells[3][..., :, None] * nearby[3][..., None, :] * (2.0 * PAIR_SCALE) / (own_cells[4][..., :, None] + nearby[4][..., None, :])
    return falloff * falloff * pairing


def diag_block(padded):
    own_cells = near_view(padded, 0, 0)
    summed = jnp.zeros(own_cells.shape[1:], jnp.float32)
    for step_x, step_y in NEIGHBOUR_STEPS:
        summed = summed + jnp.sum(pair_weights(padded, step_x, step_y), axis=-1)
    return BASE_STIFF + summed


def apply_block(padded, padded_field):
    own_cells = near_view(padded, 0, 0)
    summed = jnp.zeros(own_cells.shape[1:], jnp.float32)
    for step_x, step_y in NEIGHBOUR_STEPS:
        summed = summed + jnp.einsum('xyij,xyj->xyi', pair_weights(padded, step_x, step_y), near_view(padded_field, step_x, step_y), precision=lax.Precision.HIGHEST)
    return summed


def reference(offsets, masses, counts, source):
    slot_count = offsets.shape[-1]
    occupied = (jnp.arange(slot_count, dtype=jnp.int32)[None, None, :] < counts[:, :, None]).astype(jnp.float32)
    fields = jnp.stack([offsets[0], offsets[1], masses * occupied, occupied])
    padded = jnp.pad(fields, ((0, 0), (1, 1), (1, 1), (0, 0)))
    row_ids = jnp.arange(fields.shape[1], dtype=jnp.int32)
    density = lax.map(lambda row_index: density_block(lax.dynamic_slice_in_dim(padded, row_index, 3, 1))[0], row_ids)
    full = jnp.concatenate([padded, jnp.pad(density, ((1, 1), (1, 1), (0, 0)))[None]], 0)
    diagonal = lax.map(lambda row_index: diag_block(lax.dynamic_slice_in_dim(full, row_index, 3, 1))[0], row_ids)

    def operate(vector):
        padded_field = jnp.pad(vector, ((1, 1), (1, 1), (0, 0)))
        sums = lax.map(lambda row_index: apply_block(lax.dynamic_slice_in_dim(full, row_index, 3, 1), lax.dynamic_slice_in_dim(padded_field, row_index, 3, 0))[0], row_ids)
        return diagonal * vector - sums

    pressure = jnp.zeros_like(source)
    residual = source * occupied
    scaled = residual / diagonal
    direction = scaled
    precond_now = jnp.sum(residual * scaled)
    peak_list = []
    for step in range(ITERS):
        image = operate(direction)
        step_size = precond_now / jnp.sum(direction * image)
        pressure = pressure + step_size * direction
        residual = residual - step_size * image
        peak_list.append(jnp.max(jnp.abs(residual)))
        scaled = residual / diagonal
        precond_next = jnp.sum(residual * scaled)
        direction = scaled + (precond_next / precond_now) * direction
        precond_now = precond_next
    return density, pressure, residual, jnp.stack(peak_list)
```

```python
import jax
import jax.numpy as jnp
from jax import lax
from jax.experimental import pallas as pl
from jax.experimental.pallas import tpu as pltpu
from jax.sharding import PartitionSpec as P

ITERS = 5
BASE_STIFF = 0.5
PAIR_SCALE = 0.05
STEPS = [(sx, sy) for sx in (-1, 0, 1) for sy in (-1, 0, 1)]
DEPTH = 1
CHUNK = 32
SHIFTS = (1.0, 0.15, 0.55, 0.8, 0.3)
SCALE = 0.3
GRAM = [(i, j) for i in range(ITERS + 1) for j in range(i, ITERS + 1)]
GRAM_ROWS = -(-len(GRAM) // 8) * 8
LIMIT = pltpu.CompilerParams(vmem_limit_bytes=56 * 1024 * 1024)


def extended(block, axis, dim, width):
    count = lax.axis_size(axis)
    size = block.shape[dim]
    lows, highs = [], []
    hop, left = 1, width
    while left > 0:
        take = min(size, left)
        up = [(i, i + hop) for i in range(count - hop)]
        down = [(i + hop, i) for i in range(count - hop)]
        tail = lax.slice_in_dim(block, size - take, size, axis=dim)
        head = lax.slice_in_dim(block, 0, take, axis=dim)
        lows.insert(0, lax.ppermute(tail, axis, up))
        highs.append(lax.ppermute(head, axis, down))
        hop, left = hop + 1, left - take
    return jnp.concatenate(lows + [block] + highs, axis=dim)


def ghosted(block, width):
    rank = block.ndim
    return extended(extended(block, "gx", rank - 3, width), "gy", rank - 2, width)


def combined(part, combine):
    for axis in ("gx", "gy"):
        count = lax.axis_size(axis)
        window = 1
        while window < count:
            radix = next(k for k in (4, 2, 3, count // window) if (count // window) % k == 0)
            got = [part]
            for k in range(1, radix):
                pairs = [(i, (i + k * window) % count) for i in range(count)]
                got.append(lax.ppermute(part, axis, pairs))
            part = got[0]
            for other in got[1:]:
                part = combine(part, other)
            window *= radix
    return part


def column(row):
    slots = row.shape[-1]
    return jnp.broadcast_to(row, (slots, slots)).T


def folded(parts):
    return jnp.sum(jnp.concatenate(parts, axis=0).T, axis=0, keepdims=True)


def loop_cells(rows, cols, visit):
    def outer(r, carry):
        def inner(c, carry):
            visit(r, c)
            return carry
        return lax.fori_loop(0, cols, inner, carry)
    lax.fori_loop(0, rows, outer, 0)


def setup_kernel(f_ref, dens_ref, w_ref, aux_ref, u_ref, full_ref):
    _, rows_all, cols_all, slots = f_ref.shape
    halo = DEPTH + 2
    rows, cols = rows_all - 2 * halo, cols_all - 2 * halo

    def field(k, r, c):
        return f_ref[k, r, pl.ds(c, 1), :]

    def falloff(xc, yc, r, c, sx, sy):
        dx = (sx + field(0, r + sx, c + sy)) - xc
        dy = (sy + field(1, r + sx, c + sy)) - yc
        return jnp.maximum(1.0 - (dx * dx + dy * dy), 0.0)

    def density(r0, c0):
        r, c = r0 + 1, c0 + 1
        xc, yc = column(field(0, r, c)), column(field(1, r, c))
        parts = []
        for s in range(0, slots, CHUNK):
            acc = jnp.zeros((CHUNK, slots), jnp.float32)
            for sx, sy in STEPS:
                f = falloff(xc[s:s + CHUNK], yc[s:s + CHUNK], r, c, sx, sy)
                acc = acc + f * f * f * field(2, r + sx, c + sy)
            parts.append(acc)
        full_ref[r, pl.ds(c, 1), :] = 1.0 + folded(parts)

    loop_cells(rows_all - 2, cols_all - 2, density)

    def weights(r0, c0):
        r, c = r0 + 2, c0 + 2
        cell = r0 * (cols + 2 * DEPTH) + c0
        xc, yc = column(field(0, r, c)), column(field(1, r, c))
        dc = column(full_ref[r, pl.ds(c, 1), :])
        parts = []
        for s in range(0, slots, CHUNK):
            acc = jnp.zeros((CHUNK, slots), jnp.float32)
            for k, (sx, sy) in enumerate(STEPS):
                f = falloff(xc[s:s + CHUNK], yc[s:s + CHUNK], r, c, sx, sy)
                near = full_ref[r + sx, pl.ds(c + sy, 1), :]
                weight = f * f * (2.0 * PAIR_SCALE) / (dc[s:s + CHUNK] + near)
                w_ref[cell, k, s:s + CHUNK, :] = weight
                live = jnp.where(field(2, r + sx, c + sy) > 0.0, 1.0, 0.0)
                acc = acc + weight * live
            parts.append(acc)
        occupied = jnp.where(field(2, r, c) > 0.0, 1.0, 0.0)
        diagonal = BASE_STIFF + occupied * folded(parts)
        aux_ref[0, r0, pl.ds(c0, 1), :] = diagonal
        aux_ref[1, r0, pl.ds(c0, 1), :] = occupied / diagonal
        u_ref[r0, pl.ds(c0, 1), :] = field(3, r, c) / diagonal

    loop_cells(rows + 2 * DEPTH, cols + 2 * DEPTH, weights)
    dens_ref[...] = full_ref[halo:halo + rows, halo:halo + cols, :]


def product(w_ref, aux_ref, u_ref, out_ref, reach, shift):
    rows, cols, slots = out_ref.shape
    skip = DEPTH - reach
    span = aux_ref.shape[2]

    def visit(r, c):
        cell = (r + skip) * span + (c + skip)
        acc = jnp.zeros((slots, slots), jnp.float32)
        for k, (sx, sy) in enumerate(STEPS):
            acc = acc + w_ref[cell, k] * u_ref[r + 1 + sx, pl.ds(c + 1 + sy, 1), :]
        summed = jnp.sum(acc.T, axis=0, keepdims=True)
        own = u_ref[r + 1, pl.ds(c + 1, 1), :]
        out_ref[r, pl.ds(c, 1), :] = (
            (1.0 - shift) * own - summed * aux_ref[1, r + skip, pl.ds(c + skip, 1), :]
        ) * (1.0 / SCALE)

    loop_cells(rows, cols, visit)


def own_part(ref, rows, cols):
    edge = (ref.shape[-3] - rows) // 2
    if edge == 0:
        return ref[...]
    return ref[..., edge:edge + rows, edge:edge + cols, :]


def products_kernel(first, count, last, *refs):
    w_ref, aux_ref, u_ref = refs[:3]
    earlier = refs[3:3 + (first + 1 if last else 0)]
    tail = refs[3 + len(earlier):]
    outs = tail[:count]
    grids = tail[count + (1 if last else 0):]
    rows, cols, slots = outs[0].shape
    source = u_ref
    for n in range(count):
        reach = count - 1 - n
        target = outs[n] if reach == 0 else grids[n]
        product(w_ref, aux_ref, source, target, reach, SHIFTS[first + n])
        if reach:
            outs[n][...] = own_part(target, rows, cols)
        source = target
    if last:
        gram_ref = tail[count]
        diagonal = own_part(aux_ref, rows, cols)[0]
        basis = [own_part(r, rows, cols) for r in earlier] + [r[...] for r in outs]
        lines = []
        for i, j in GRAM:
            term = basis[i] * basis[j] * diagonal
            lines.append(jnp.sum(jnp.sum(term, axis=0), axis=0, keepdims=True))
        lines += [jnp.zeros((1, slots), jnp.float32)] * (GRAM_ROWS - len(GRAM))
        gram_ref[...] = jnp.concatenate(lines, axis=0)


def solve_kernel(gram_ref, aux_ref, *refs):
    basis_refs = refs[:ITERS + 1]
    pressure_ref, residual_ref, peak_ref = refs[ITERS + 1:]
    rows, cols, slots = pressure_ref.shape
    totals = jnp.sum(gram_ref[...], axis=1, keepdims=True)
    gram = {}
    for n, (i, j) in enumerate(GRAM):
        gram[i, j] = gram[j, i] = totals[n:n + 1, :]
    zero = jnp.zeros((1, 1), jnp.float32)

    def mapped(v):
        out = [None] * (len(v) + 1)
        for k in range(len(v) + 1):
            term = SHIFTS[k] * v[k] if k < len(v) else zero
            out[k] = term + (SCALE * v[k - 1] if k else zero)
        return out

    def inner(a, b):
        total = zero
        for i, ai in enumerate(a):
            line = zero
            for j, bj in enumerate(b):
                line = line + gram[i, j] * bj
            total = total + ai * line
        return total

    def added(a, b, scale):
        size = max(len(a), len(b))
        pad = lambda v: v + [zero] * (size - len(v))
        return [x + scale * y for x, y in zip(pad(a), pad(b))]

    diagonal = own_part(aux_ref, rows, cols)[0]
    basis = [own_part(r, rows, cols) for r in basis_refs]

    def expand(coefs):
        total = None
        for k, coef in enumerate(coefs):
            term = coef.reshape(1, 1, 1) * basis[k]
            total = term if total is None else total + term
        return total

    z = [jnp.ones((1, 1), jnp.float32)]
    p = list(z)
    x = []
    rz = inner(z, z)
    tops = []
    for step in range(ITERS):
        image = mapped(p)
        size = rz / inner(p, image)
        x = added(x, p, size)
        z = added(z, image, -size)
        residual = diagonal * expand(z)
        tops.append(jnp.max(jnp.max(jnp.abs(residual), axis=0), axis=0, keepdims=True))
        if step + 1 < ITERS:
            following = inner(z, z)
            p = added(z, p, following / rz)
            rz = following
    pressure_ref[...] = expand(x)
    residual_ref[...] = residual
    tops += [jnp.zeros((1, slots), jnp.float32)] * (8 - len(tops))
    peak = jnp.max(jnp.concatenate(tops, axis=0), axis=1, keepdims=True)
    peak_ref[...] = jnp.broadcast_to(peak, (8, slots))


def body(offsets, masses, counts, source):
    _, rows, cols, slots = offsets.shape
    f32 = jnp.float32
    live = jnp.arange(slots, dtype=jnp.int32)[None, None, :] < counts[:, :, None]
    fields = jnp.concatenate(
        [offsets, jnp.where(live, masses, 0.0)[None], jnp.where(live, source, 0.0)[None]]
    )
    padded = ghosted(fields, DEPTH + 2)
    span_r, span_c = rows + 2 * DEPTH, cols + 2 * DEPTH
    own = jax.ShapeDtypeStruct((rows, cols, slots), f32)
    density, weight, aux, vector = pl.pallas_call(
        setup_kernel,
        out_shape=(
            own,
            WEIGHT_SPACE((span_r * span_c, len(STEPS), slots, slots), f32),
            jax.ShapeDtypeStruct((2, span_r, span_c, slots), f32),
            jax.ShapeDtypeStruct((span_r, span_c, slots), f32),
        ),
        scratch_shapes=[pltpu.VMEM(padded.shape[1:], f32)],
        compiler_params=LIMIT,
        name="setup",
    )(padded)
    basis = [vector]
    wide = vector
    reach = DEPTH
    while len(basis) <= ITERS:
        if reach == 0:
            reach = min(DEPTH + 1, ITERS + 1 - len(basis))
            wide = ghosted(basis[-1], reach)
        first = len(basis) - 1
        count = reach
        last = first + count == ITERS
        outs = [own] * count
        if last:
            outs.append(jax.ShapeDtypeStruct((GRAM_ROWS, slots), f32))
        grids = [
            pltpu.VMEM((rows + 2 * e, cols + 2 * e, slots), f32) for e in range(count - 1, 0, -1)
        ]
        got = pl.pallas_call(
            lambda *refs, a=first, n=count, z=last: products_kernel(a, n, z, *refs),
            out_shape=tuple(outs),
            scratch_shapes=grids,
            compiler_params=LIMIT,
            name=f"products_{first}",
        )(weight, aux, wide, *(basis if last else []))
        basis += list(got[:count])
        if last:
            gram = got[count]
        reach = 0
    gram = combined(gram, jnp.add)
    pressure, residual, peak = pl.pallas_call(
        solve_kernel,
        out_shape=(own, own, jax.ShapeDtypeStruct((8, slots), f32)),
        compiler_params=LIMIT,
        name="solve",
    )(gram, aux, *basis)
    peak = combined(peak, jnp.maximum)
    return density, pressure, residual, peak[:ITERS, 0]


WEIGHT_SPACE = jax.ShapeDtypeStruct


def solution(mesh):
    in_specs = (P(None, "gx", "gy", None), P("gx", "gy", None), P("gx", "gy"), P("gx", "gy", None))
    out_specs = (P("gx", "gy", None), P("gx", "gy", None), P("gx", "gy", None), P())
    return jax.shard_map(body, mesh=mesh, in_specs=in_specs, out_specs=out_specs, check_vma=False)
```

```python
import jax
import jax.numpy as jnp
from jax import lax
from jax.experimental import pallas as pl
from jax.experimental.pallas import tpu as pltpu
from jax.sharding import PartitionSpec as P

ITERS = 5
BASE_STIFF = 0.5
PAIR_SCALE = 0.05
STEPS = [(sx, sy) for sx in (-1, 0, 1) for sy in (-1, 0, 1)]
DEPTH = 1
CHUNK = 32
SHIFTS = (1.0, 0.15, 0.55, 0.8, 0.3)
SCALE = 0.3
GRAM = [(i, j) for i in range(ITERS + 1) for j in range(i, ITERS + 1)]
GRAM_ROWS = -(-len(GRAM) // 8) * 8
LIMIT = pltpu.CompilerParams(vmem_limit_bytes=12 * 1024 * 1024)


def extended(block, axis, dim, width):
    count = lax.axis_size(axis)
    size = block.shape[dim]
    lows, highs = [], []
    hop, left = 1, width
    while left > 0:
        take = min(size, left)
        up = [(i, i + hop) for i in range(count - hop)]
        down = [(i + hop, i) for i in range(count - hop)]
        tail = lax.slice_in_dim(block, size - take, size, axis=dim)
        head = lax.slice_in_dim(block, 0, take, axis=dim)
        lows.insert(0, lax.ppermute(tail, axis, up))
        highs.append(lax.ppermute(head, axis, down))
        hop, left = hop + 1, left - take
    return jnp.concatenate(lows + [block] + highs, axis=dim)


def ghosted(block, width):
    rank = block.ndim
    return extended(extended(block, "gx", rank - 3, width), "gy", rank - 2, width)


def combined(part, combine):
    for axis in ("gx", "gy"):
        count = lax.axis_size(axis)
        window = 1
        while window < count:
            radix = next(k for k in (4, 2, 3, count // window) if (count // window) % k == 0)
            got = [part]
            for k in range(1, radix):
                pairs = [(i, (i + k * window) % count) for i in range(count)]
                got.append(lax.ppermute(part, axis, pairs))
            part = got[0]
            for other in got[1:]:
                part = combine(part, other)
            window *= radix
    return part


def column(row):
    slots = row.shape[-1]
    return jnp.broadcast_to(row, (slots, slots)).T


def folded(parts):
    return jnp.sum(jnp.concatenate(parts, axis=0).T, axis=0, keepdims=True)


def loop_cells(rows, cols, visit):
    def outer(r, carry):
        def inner(c, carry):
            visit(r, c)
            return carry
        return lax.fori_loop(0, cols, inner, carry)
    lax.fori_loop(0, rows, outer, 0)


def setup_kernel(f_ref, dens_ref, w_ref, aux_ref, u_ref, full_ref):
    _, rows_all, cols_all, slots = f_ref.shape
    halo = DEPTH + 2
    rows, cols = rows_all - 2 * halo, cols_all - 2 * halo

    def field(k, r, c):
        return f_ref[k, r, pl.ds(c, 1), :]

    def falloff(xc, yc, r, c, sx, sy):
        dx = (sx + field(0, r + sx, c + sy)) - xc
        dy = (sy + field(1, r + sx, c + sy)) - yc
        return jnp.maximum(1.0 - (dx * dx + dy * dy), 0.0)

    def density(r0, c0):
        r, c = r0 + 1, c0 + 1
        xc, yc = column(field(0, r, c)), column(field(1, r, c))
        parts = []
        for s in range(0, slots, CHUNK):
            acc = jnp.zeros((CHUNK, slots), jnp.float32)
            for sx, sy in STEPS:
                f = falloff(xc[s:s + CHUNK], yc[s:s + CHUNK], r, c, sx, sy)
                acc = acc + f * f * f * field(2, r + sx, c + sy)
            parts.append(acc)
        full_ref[r, pl.ds(c, 1), :] = 1.0 + folded(parts)

    loop_cells(rows_all - 2, cols_all - 2, density)

    def weights(r0, c0):
        r, c = r0 + 2, c0 + 2
        cell = r0 * (cols + 2 * DEPTH) + c0
        xc, yc = column(field(0, r, c)), column(field(1, r, c))
        dc = column(full_ref[r, pl.ds(c, 1), :])
        parts = []
        for s in range(0, slots, CHUNK):
            acc = jnp.zeros((CHUNK, slots), jnp.float32)
            for k, (sx, sy) in enumerate(STEPS):
                f = falloff(xc[s:s + CHUNK], yc[s:s + CHUNK], r, c, sx, sy)
                near = full_ref[r + sx, pl.ds(c + sy, 1), :]
                weight = f * f * (2.0 * PAIR_SCALE) / (dc[s:s + CHUNK] + near)
                w_ref[cell, k, s:s + CHUNK, :] = weight
                live = jnp.where(field(2, r + sx, c + sy) > 0.0, 1.0, 0.0)
                acc = acc + weight * live
            parts.append(acc)
        occupied = jnp.where(field(2, r, c) > 0.0, 1.0, 0.0)
        diagonal = BASE_STIFF + occupied * folded(parts)
        aux_ref[0, r0, pl.ds(c0, 1), :] = diagonal
        aux_ref[1, r0, pl.ds(c0, 1), :] = occupied / diagonal
        u_ref[r0, pl.ds(c0, 1), :] = field(3, r, c) / diagonal

    loop_cells(rows + 2 * DEPTH, cols + 2 * DEPTH, weights)
    dens_ref[...] = full_ref[halo:halo + rows, halo:halo + cols, :]


def product(w_ref, aux_ref, u_ref, out_ref, reach, shift):
    rows, cols, slots = out_ref.shape
    skip = DEPTH - reach
    span = aux_ref.shape[2]

    def visit(r, c):
        cell = (r + skip) * span + (c + skip)
        acc = jnp.zeros((slots, slots), jnp.float32)
        for k, (sx, sy) in enumerate(STEPS):
            acc = acc + w_ref[cell, k] * u_ref[r + 1 + sx, pl.ds(c + 1 + sy, 1), :]
        summed = jnp.sum(acc.T, axis=0, keepdims=True)
        own = u_ref[r + 1, pl.ds(c + 1, 1), :]
        out_ref[r, pl.ds(c, 1), :] = (
            (1.0 - shift) * own - summed * aux_ref[1, r + skip, pl.ds(c + skip, 1), :]
        ) * (1.0 / SCALE)

    loop_cells(rows, cols, visit)


def own_part(ref, rows, cols):
    edge = (ref.shape[-3] - rows) // 2
    if edge == 0:
        return ref[...]
    return ref[..., edge:edge + rows, edge:edge + cols, :]


def products_kernel(first, count, last, *refs):
    w_ref, aux_ref, u_ref = refs[:3]
    earlier = refs[3:3 + (first + 1 if last else 0)]
    tail = refs[3 + len(earlier):]
    outs = tail[:count]
    grids = tail[count + (1 if last else 0):]
    rows, cols, slots = outs[0].shape
    source = u_ref
    for n in range(count):
        reach = count - 1 - n
        target = outs[n] if reach == 0 else grids[n]
        product(w_ref, aux_ref, source, target, reach, SHIFTS[first + n])
        if reach:
            outs[n][...] = own_part(target, rows, cols)
        source = target
    if last:
        gram_ref = tail[count]
        diagonal = own_part(aux_ref, rows, cols)[0]
        basis = [own_part(r, rows, cols) for r in earlier] + [r[...] for r in outs]
        lines = []
        for i, j in GRAM:
            term = basis[i] * basis[j] * diagonal
            lines.append(jnp.sum(jnp.sum(term, axis=0), axis=0, keepdims=True))
        lines += [jnp.zeros((1, slots), jnp.float32)] * (GRAM_ROWS - len(GRAM))
        gram_ref[...] = jnp.concatenate(lines, axis=0)


def solve_kernel(gram_ref, aux_ref, *refs):
    basis_refs = refs[:ITERS + 1]
    pressure_ref, residual_ref, peak_ref = refs[ITERS + 1:]
    rows, cols, slots = pressure_ref.shape
    totals = jnp.sum(gram_ref[...], axis=1, keepdims=True)
    gram = {}
    for n, (i, j) in enumerate(GRAM):
        gram[i, j] = gram[j, i] = totals[n:n + 1, :]
    zero = jnp.zeros((1, 1), jnp.float32)

    def mapped(v):
        out = [None] * (len(v) + 1)
        for k in range(len(v) + 1):
            term = SHIFTS[k] * v[k] if k < len(v) else zero
            out[k] = term + (SCALE * v[k - 1] if k else zero)
        return out

    def inner(a, b):
        total = zero
        for i, ai in enumerate(a):
            line = zero
            for j, bj in enumerate(b):
                line = line + gram[i, j] * bj
            total = total + ai * line
        return total

    def added(a, b, scale):
        size = max(len(a), len(b))
        pad = lambda v: v + [zero] * (size - len(v))
        return [x + scale * y for x, y in zip(pad(a), pad(b))]

    diagonal = own_part(aux_ref, rows, cols)[0]
    basis = [own_part(r, rows, cols) for r in basis_refs]

    def expand(coefs):
        total = None
        for k, coef in enumerate(coefs):
            term = coef.reshape(1, 1, 1) * basis[k]
            total = term if total is None else total + term
        return total

    z = [jnp.ones((1, 1), jnp.float32)]
    p = list(z)
    x = []
    rz = inner(z, z)
    tops = []
    for step in range(ITERS):
        image = mapped(p)
        size = rz / inner(p, image)
        x = added(x, p, size)
        z = added(z, image, -size)
        residual = diagonal * expand(z)
        tops.append(jnp.max(jnp.max(jnp.abs(residual), axis=0), axis=0, keepdims=True))
        if step + 1 < ITERS:
            following = inner(z, z)
            p = added(z, p, following / rz)
            rz = following
    pressure_ref[...] = expand(x)
    residual_ref[...] = residual
    tops += [jnp.zeros((1, slots), jnp.float32)] * (8 - len(tops))
    peak = jnp.max(jnp.concatenate(tops, axis=0), axis=1, keepdims=True)
    peak_ref[...] = jnp.broadcast_to(peak, (8, slots))


def body(offsets, masses, counts, source):
    _, rows, cols, slots = offsets.shape
    f32 = jnp.float32
    live = jnp.arange(slots, dtype=jnp.int32)[None, None, :] < counts[:, :, None]
    fields = jnp.concatenate(
        [offsets, jnp.where(live, masses, 0.0)[None], jnp.where(live, source, 0.0)[None]]
    )
    padded = ghosted(fields, DEPTH + 2)
    span_r, span_c = rows + 2 * DEPTH, cols + 2 * DEPTH
    own = jax.ShapeDtypeStruct((rows, cols, slots), f32)
    density, weight, aux, vector = pl.pallas_call(
        setup_kernel,
        out_shape=(
            own,
            WEIGHT_SPACE((span_r * span_c, len(STEPS), slots, slots), f32),
            jax.ShapeDtypeStruct((2, span_r, span_c, slots), f32),
            jax.ShapeDtypeStruct((span_r, span_c, slots), f32),
        ),
        scratch_shapes=[pltpu.VMEM(padded.shape[1:], f32)],
        compiler_params=LIMIT,
        name="setup",
    )(padded)
    kept = weight
    basis = [vector]
    wide = vector
    reach = DEPTH
    while len(basis) <= ITERS:
        if reach == 0:
            reach = min(DEPTH + 1, ITERS + 1 - len(basis))
            wide = ghosted(basis[-1], reach)
        first = len(basis) - 1
        count = reach
        last = first + count == ITERS
        outs = [own] * count
        if last:
            outs.append(jax.ShapeDtypeStruct((GRAM_ROWS, slots), f32))
        grids = [
            pltpu.VMEM((rows + 2 * e, cols + 2 * e, slots), f32) for e in range(count - 1, 0, -1)
        ]
        got = pl.pallas_call(
            lambda *refs, a=first, n=count, z=last: products_kernel(a, n, z, *refs),
            out_shape=tuple(outs),
            scratch_shapes=grids,
            compiler_params=LIMIT,
            name=f"products_{first}",
        )(kept, aux, wide, *(basis if last else []))
        basis += list(got[:count])
        if last:
            gram = got[count]
        reach = 0
    gram = combined(gram, jnp.add)
    pressure, residual, peak = pl.pallas_call(
        solve_kernel,
        out_shape=(own, own, jax.ShapeDtypeStruct((8, slots), f32)),
        compiler_params=LIMIT,
        name="solve",
    )(gram, aux, *basis)
    peak = combined(peak, jnp.maximum)
    return density, pressure, residual, peak[:ITERS, 0]


WEIGHT_SPACE = jax.ShapeDtypeStruct


def solution(mesh):
    in_specs = (P(None, "gx", "gy", None), P("gx", "gy", None), P("gx", "gy"), P("gx", "gy", None))
    out_specs = (P("gx", "gy", None), P("gx", "gy", None), P("gx", "gy", None), P())
    return jax.shard_map(body, mesh=mesh, in_specs=in_specs, out_specs=out_specs, check_vma=False)
```

```python
import functools

import jax
import jax.numpy as jnp
import numpy as np
from jax import lax
from jax.experimental import pallas as pl
from jax.experimental.pallas import tpu as pltpu
from jax.sharding import PartitionSpec as P

ITERS = 5
BASE_STIFF = 0.5
PAIR_SCALE = 0.05
STEPS = [(sx, sy) for sx in (-1, 0, 1) for sy in (-1, 0, 1)]
DEPTH = 1
SPLIT_ROWS = 32
DEAD = -1.0e6
SHIFTS = (1.0, 0.15, 0.55, 0.8, 0.3)
SCALE = 0.3
GRAM = [(i, j) for i in range(ITERS + 1) for j in range(i, ITERS + 1)]
GRAM_ROWS = -(-len(GRAM) // 8) * 8
LIMIT = pltpu.CompilerParams(vmem_limit_bytes=12 * 1024 * 1024)


def extended(block, axis, dim, width):
    count = lax.axis_size(axis)
    size = block.shape[dim]
    lows, highs = [], []
    hop, left = 1, width
    while left > 0:
        take = min(size, left)
        up = [(i, i + hop) for i in range(count - hop)]
        down = [(i + hop, i) for i in range(count - hop)]
        tail = lax.slice_in_dim(block, size - take, size, axis=dim)
        head = lax.slice_in_dim(block, 0, take, axis=dim)
        lows.insert(0, lax.ppermute(tail, axis, up))
        highs.append(lax.ppermute(head, axis, down))
        hop, left = hop + 1, left - take
    return jnp.concatenate(lows + [block] + highs, axis=dim)


def ghosted(block, width):
    rank = block.ndim
    return extended(extended(block, "gx", rank - 3, width), "gy", rank - 2, width)


def combined(part, combine):
    for axis in ("gx", "gy"):
        count = lax.axis_size(axis)
        window = 1
        while window < count:
            radix = next(k for k in (4, 2, 3, count // window) if (count // window) % k == 0)
            got = [part]
            for k in range(1, radix):
                group = radix * window
                pairs = [
                    (i, i // group * group + (i % group + k * window) % group)
                    for i in range(count)
                ]
                got.append(lax.ppermute(part, axis, pairs))
            part = got[0]
            for other in got[1:]:
                part = combine(part, other)
            window *= radix
    return part


def column(row):
    slots = row.shape[-1]
    return jnp.broadcast_to(row, (slots, slots)).T


def loop_cells(row_from, row_to, col_from, col_to, visit):
    def outer(r, carry):
        def inner(c, carry):
            visit(r, c)
            return carry
        return lax.fori_loop(col_from, col_to, inner, carry, unroll=min(2, col_to - col_from))
    lax.fori_loop(row_from, row_to, outer, 0)


def split_tables(slots):
    pairs = ((0, 0), (0, 1), (1, 0), (1, 1), (0, 2), (2, 0))
    left = [(0, 1.0), (1, 1.0), (2, 1.0), (3, 1.0), (3, 1.0), (3, 1.0)]
    right = [(3, 1.0), (3, 1.0), (3, 1.0), (0, 1.0), (1, 1.0), (2, 1.0)]
    for _ in range(2):
        left += [(p, 2.0) for p, _ in pairs]
        right += [(q, 1.0) for _, q in pairs]
    table = np.zeros((8, SPLIT_ROWS, slots), np.float32)
    for row, ((p, x), (q, y)) in enumerate(zip(left, right)):
        table[p, row], table[4 + q, row] = x, y
    return table


def setup_kernel(f_ref, table_ref, dens_ref, w_ref, aux_ref, u_ref, full_ref, inv_ref, a_ref, b_ref):
    _, rows_all, cols_all, slots = f_ref.shape
    halo = DEPTH + 2
    rows, cols = rows_all - 2 * halo, cols_all - 2 * halo
    span = cols + 2 * DEPTH
    kind = lax.broadcasted_iota(jnp.int32, (SPLIT_ROWS, slots), 0)

    def field(k, r, c):
        return f_ref[k, r, pl.ds(c, 1), :]

    def factors(r, c):
        x = field(0, r, c) + (jnp.float32(r) - 0.5 * rows_all)
        y = field(1, r, c) + (jnp.float32(c) - 0.5 * cols_all)
        own = 0.5 - (x * x + y * y)
        near = jnp.where(field(2, r, c) > 0.0, own, DEAD)
        x, y = (jnp.broadcast_to(v, kind.shape) for v in (x, y))

        def parts(first, base):
            value = jnp.where(kind < 6, first, jnp.where(kind < 12, x, y))
            high = value.astype(jnp.bfloat16).astype(jnp.float32)
            rest = value - high
            middle = rest.astype(jnp.bfloat16).astype(jnp.float32)
            low = rest - middle
            total = (
                high * table_ref[base] + middle * table_ref[base + 1]
                + low * table_ref[base + 2] + table_ref[base + 3]
            )
            return total.astype(jnp.bfloat16)

        a_ref[r * cols_all + c] = parts(own, 0)
        b_ref[r * cols_all + c] = parts(near, 4)

    loop_cells(0, rows_all, 0, cols_all, factors)

    def density(keep, r, c):
        acc = jnp.zeros((slots, slots), jnp.float32)
        left = a_ref[r * cols_all + c]
        cell = (r - 2) * span + (c - 2)
        for k, (sx, sy) in enumerate(STEPS):
            f = lax.dot_general(
                left, b_ref[(r + sx) * cols_all + c + sy], (((0,), (0,)), ((), ())),
                preferred_element_type=jnp.float32,
            )
            f = jnp.maximum(f, 0.0)
            square = f * f
            if keep:
                w_ref[cell, k] = square
            acc = acc + square * (f * field(2, r + sx, c + sy))
        value = 1.0 + jnp.sum(acc.T, axis=0, keepdims=True)
        full_ref[r, pl.ds(c, 1), :] = value
        inv_ref[r, pl.ds(c, 1), :] = value * (1.0 / (2.0 * PAIR_SCALE))

    kept, edge = functools.partial(density, True), functools.partial(density, False)
    loop_cells(2, rows_all - 2, 2, cols_all - 2, kept)
    for r in (1, rows_all - 2):
        loop_cells(r, r + 1, 1, cols_all - 1, edge)
    for c in (1, cols_all - 2):
        loop_cells(2, rows_all - 2, c, c + 1, edge)

    def weights(r, c):
        r0, c0 = r - 2, c - 2
        cell = r0 * span + c0
        dc = column(inv_ref[r, pl.ds(c, 1), :])
        acc = jnp.zeros((slots, slots), jnp.float32)
        for k, (sx, sy) in enumerate(STEPS):
            near = inv_ref[r + sx, pl.ds(c + sy, 1), :]
            weight = w_ref[cell, k] * pl.reciprocal(dc + near)
            w_ref[cell, k] = weight
            acc = acc + weight
        occupied = jnp.where(field(2, r, c) > 0.0, 1.0, 0.0)
        diagonal = BASE_STIFF + occupied * jnp.sum(acc.T, axis=0, keepdims=True)
        aux_ref[0, r0, pl.ds(c0, 1), :] = diagonal
        aux_ref[1, r0, pl.ds(c0, 1), :] = occupied / diagonal
        u_ref[r0, pl.ds(c0, 1), :] = field(3, r, c) / diagonal

    loop_cells(2, rows_all - 2, 2, cols_all - 2, weights)
    dens_ref[...] = full_ref[halo:halo + rows, halo:halo + cols, :]


def product(w_ref, aux_ref, u_ref, out_ref, reach, shift):
    rows, cols, slots = out_ref.shape
    skip = DEPTH - reach
    span = aux_ref.shape[2]

    def visit(r, c):
        cell = (r + skip) * span + (c + skip)
        acc = jnp.zeros((slots, slots), jnp.float32)
        for k, (sx, sy) in enumerate(STEPS):
            acc = acc + w_ref[cell, k] * u_ref[r + 1 + sx, pl.ds(c + 1 + sy, 1), :]
        summed = jnp.sum(acc.T, axis=0, keepdims=True)
        own = u_ref[r + 1, pl.ds(c + 1, 1), :]
        out_ref[r, pl.ds(c, 1), :] = (
            (1.0 - shift) * own - summed * aux_ref[1, r + skip, pl.ds(c + skip, 1), :]
        ) * (1.0 / SCALE)

    loop_cells(0, rows, 0, cols, visit)


def own_part(ref, rows, cols):
    edge = (ref.shape[-3] - rows) // 2
    if edge == 0:
        return ref[...]
    return ref[..., edge:edge + rows, edge:edge + cols, :]


def products_kernel(first, count, last, *refs):
    w_ref, aux_ref, u_ref = refs[:3]
    earlier = refs[3:3 + (first + 1 if last else 0)]
    tail = refs[3 + len(earlier):]
    outs = tail[:count]
    grids = tail[count + (1 if last else 0):]
    rows, cols, slots = outs[0].shape
    source = u_ref
    for n in range(count):
        reach = count - 1 - n
        target = outs[n] if reach == 0 else grids[n]
        product(w_ref, aux_ref, source, target, reach, SHIFTS[first + n])
        if reach:
            outs[n][...] = own_part(target, rows, cols)
        source = target
    if last:
        gram_ref = tail[count]
        diagonal = own_part(aux_ref, rows, cols)[0]
        basis = [own_part(r, rows, cols) for r in earlier] + [r[...] for r in outs]
        lines = []
        for i, j in GRAM:
            term = basis[i] * basis[j] * diagonal
            lines.append(jnp.sum(jnp.sum(term, axis=0), axis=0, keepdims=True))
        lines += [jnp.zeros((1, slots), jnp.float32)] * (GRAM_ROWS - len(GRAM))
        gram_ref[...] = jnp.concatenate(lines, axis=0)


def solve_kernel(gram_ref, aux_ref, *refs):
    basis_refs = refs[:ITERS + 1]
    pressure_ref, residual_ref, peak_ref = refs[ITERS + 1:]
    rows, cols, slots = pressure_ref.shape
    totals = jnp.sum(gram_ref[...], axis=1, keepdims=True)
    gram = {}
    for n, (i, j) in enumerate(GRAM):
        gram[i, j] = gram[j, i] = totals[n:n + 1, :]
    zero = jnp.zeros((1, 1), jnp.float32)

    def mapped(v):
        out = [None] * (len(v) + 1)
        for k in range(len(v) + 1):
            term = SHIFTS[k] * v[k] if k < len(v) else zero
            out[k] = term + (SCALE * v[k - 1] if k else zero)
        return out

    def inner(a, b):
        total = zero
        for i, ai in enumerate(a):
            line = zero
            for j, bj in enumerate(b):
                line = line + gram[i, j] * bj
            total = total + ai * line
        return total

    def added(a, b, scale):
        size = max(len(a), len(b))
        pad = lambda v: v + [zero] * (size - len(v))
        return [x + scale * y for x, y in zip(pad(a), pad(b))]

    diagonal = own_part(aux_ref, rows, cols)[0]
    basis = [own_part(r, rows, cols) for r in basis_refs]

    def expand(coefs):
        total = None
        for k, coef in enumerate(coefs):
            term = coef.reshape(1, 1, 1) * basis[k]
            total = term if total is None else total + term
        return total

    z = [jnp.ones((1, 1), jnp.float32)]
    p = list(z)
    x = []
    rz = inner(z, z)
    tops = []
    for step in range(ITERS):
        image = mapped(p)
        size = rz / inner(p, image)
        x = added(x, p, size)
        z = added(z, image, -size)
        residual = diagonal * expand(z)
        tops.append(jnp.max(jnp.max(jnp.abs(residual), axis=0), axis=0, keepdims=True))
        if step + 1 < ITERS:
            following = inner(z, z)
            p = added(z, p, following / rz)
            rz = following
    pressure_ref[...] = expand(x)
    residual_ref[...] = residual
    tops += [jnp.zeros((1, slots), jnp.float32)] * (8 - len(tops))
    peak = jnp.max(jnp.concatenate(tops, axis=0), axis=1, keepdims=True)
    peak_ref[...] = jnp.broadcast_to(peak, (8, slots))


def body(offsets, masses, counts, source):
    _, rows, cols, slots = offsets.shape
    f32 = jnp.float32
    live = jnp.arange(slots, dtype=jnp.int32)[None, None, :] < counts[:, :, None]
    fields = jnp.concatenate(
        [offsets, jnp.where(live, masses, 0.0)[None], jnp.where(live, source, 0.0)[None]]
    )
    padded = ghosted(fields, DEPTH + 2)
    cells = padded.shape[1] * padded.shape[2]
    span_r, span_c = rows + 2 * DEPTH, cols + 2 * DEPTH
    own = jax.ShapeDtypeStruct((rows, cols, slots), f32)
    density, weight, aux, vector = pl.pallas_call(
        setup_kernel,
        out_shape=(
            own,
            WEIGHT_SPACE((span_r * span_c, len(STEPS), slots, slots), f32),
            jax.ShapeDtypeStruct((2, span_r, span_c, slots), f32),
            jax.ShapeDtypeStruct((span_r, span_c, slots), f32),
        ),
        scratch_shapes=[
            pltpu.VMEM(padded.shape[1:], f32),
            pltpu.VMEM(padded.shape[1:], f32),
            pltpu.VMEM((cells, SPLIT_ROWS, slots), jnp.bfloat16),
            pltpu.VMEM((cells, SPLIT_ROWS, slots), jnp.bfloat16),
        ],
        compiler_params=LIMIT,
        name="setup",
    )(padded, jnp.asarray(split_tables(slots)))
    kept = weight
    basis = [vector]
    wide = vector
    reach = DEPTH
    while len(basis) <= ITERS:
        if reach == 0:
            reach = min(DEPTH + 1, ITERS + 1 - len(basis))
            wide = ghosted(basis[-1], reach)
        first = len(basis) - 1
        count = reach
        last = first + count == ITERS
        outs = [own] * count
        if last:
            outs.append(jax.ShapeDtypeStruct((GRAM_ROWS, slots), f32))
        grids = [
            pltpu.VMEM((rows + 2 * e, cols + 2 * e, slots), f32) for e in range(count - 1, 0, -1)
        ]
        got = pl.pallas_call(
            lambda *refs, a=first, n=count, z=last: products_kernel(a, n, z, *refs),
            out_shape=tuple(outs),
            scratch_shapes=grids,
            compiler_params=LIMIT,
            name=f"products_{first}",
        )(kept, aux, wide, *(basis if last else []))
        basis += list(got[:count])
        if last:
            gram = got[count]
        reach = 0
    gram = combined(gram, jnp.add)
    pressure, residual, peak = pl.pallas_call(
        solve_kernel,
        out_shape=(own, own, jax.ShapeDtypeStruct((8, slots), f32)),
        compiler_params=LIMIT,
        name="solve",
    )(gram, aux, *basis)
    peak = combined(peak, jnp.maximum)
    return density, pressure, residual, peak[:ITERS, 0]


WEIGHT_SPACE = jax.ShapeDtypeStruct


def solution(mesh):
    in_specs = (P(None, "gx", "gy", None), P("gx", "gy", None), P("gx", "gy"), P("gx", "gy", None))
    out_specs = (P("gx", "gy", None), P("gx", "gy", None), P("gx", "gy", None), P())
    return jax.shard_map(body, mesh=mesh, in_specs=in_specs, out_specs=out_specs, check_vma=False)
```

```python
import functools

import jax
import jax.numpy as jnp
from jax import lax
from jax.experimental import pallas as pl
from jax.experimental.pallas import tpu as pltpu
from jax.sharding import PartitionSpec as P

ITERS = 5
BASE_STIFF = 0.5
PAIR_SCALE = 0.05
STEPS = [(sx, sy) for sx in (-1, 0, 1) for sy in (-1, 0, 1)]
DEPTH = 1
SPLIT_ROWS = 32
DEAD = -1.0e6
SHIFTS = (1.0, 0.15, 0.55, 0.8, 0.3)
SCALE = 0.3
GRAM = [(i, j) for i in range(ITERS + 1) for j in range(i, ITERS + 1)]
GRAM_ROWS = -(-len(GRAM) // 8) * 8
LIMIT = pltpu.CompilerParams(vmem_limit_bytes=12 * 1024 * 1024)


def extended(block, axis, dim, width):
    count = lax.axis_size(axis)
    size = block.shape[dim]
    lows, highs = [], []
    hop, left = 1, width
    while left > 0:
        take = min(size, left)
        up = [(i, i + hop) for i in range(count - hop)]
        down = [(i + hop, i) for i in range(count - hop)]
        tail = lax.slice_in_dim(block, size - take, size, axis=dim)
        head = lax.slice_in_dim(block, 0, take, axis=dim)
        lows.insert(0, lax.ppermute(tail, axis, up))
        highs.append(lax.ppermute(head, axis, down))
        hop, left = hop + 1, left - take
    return jnp.concatenate(lows + [block] + highs, axis=dim)


def ghosted(block, width):
    rank = block.ndim
    return extended(extended(block, "gx", rank - 3, width), "gy", rank - 2, width)


def combined(part, combine):
    for axis in ("gx", "gy"):
        count = lax.axis_size(axis)
        window = 1
        while window < count:
            radix = next(k for k in (8, 4, 2, 3, count // window) if (count // window) % k == 0)
            got = [part]
            for k in range(1, radix):
                group = radix * window
                pairs = [
                    (i, i // group * group + (i % group + k * window) % group)
                    for i in range(count)
                ]
                got.append(lax.ppermute(part, axis, pairs))
            part = got[0]
            for other in got[1:]:
                part = combine(part, other)
            window *= radix
    return part


def column(row):
    slots = row.shape[-1]
    return jnp.broadcast_to(row, (slots, slots)).T


def loop_cells(row_from, row_to, col_from, col_to, visit, most=2):
    count = col_to - col_from
    unroll = max(k for k in range(1, most + 1) if count % k == 0)

    def outer(r, carry):
        def inner(c, carry):
            visit(r, c)
            return carry
        return lax.fori_loop(col_from, col_to, inner, carry, unroll=unroll)
    lax.fori_loop(row_from, row_to, outer, 0)


def write_tables(table_ref, kind):
    pairs = ((0, 0), (0, 1), (1, 0), (1, 1), (0, 2), (2, 0))
    left = [(0, 1.0), (1, 1.0), (2, 1.0), (3, 1.0), (3, 1.0), (3, 1.0)]
    right = [(3, 1.0), (3, 1.0), (3, 1.0), (0, 1.0), (1, 1.0), (2, 1.0)]
    for _ in range(2):
        left += [(p, 2.0) for p, _ in pairs]
        right += [(q, 1.0) for _, q in pairs]
    for base, side in ((0, left), (4, right)):
        for part in range(4):
            value = jnp.zeros(kind.shape, jnp.float32)
            for row, (p, scale) in enumerate(side):
                if p == part:
                    value = jnp.where(kind == row, scale, value)
            table_ref[base + part] = value


def setup_kernel(f_ref, dens_ref, w_ref, aux_ref, u_ref, full_ref, inv_ref, a_ref, b_ref, table_ref):
    _, rows_all, cols_all, slots = f_ref.shape
    halo = DEPTH + 2
    rows, cols = rows_all - 2 * halo, cols_all - 2 * halo
    span = cols + 2 * DEPTH
    kind = lax.broadcasted_iota(jnp.int32, (SPLIT_ROWS, slots), 0)
    write_tables(table_ref, kind)

    def field(k, r, c):
        return f_ref[k, r, pl.ds(c, 1), :]

    def factors(r, c):
        x = field(0, r, c) + (jnp.float32(r) - 0.5 * rows_all)
        y = field(1, r, c) + (jnp.float32(c) - 0.5 * cols_all)
        own = 0.5 - (x * x + y * y)
        near = jnp.where(field(2, r, c) > 0.0, own, DEAD)
        x, y = (jnp.broadcast_to(v, kind.shape) for v in (x, y))

        def parts(first, base):
            value = jnp.where(kind < 6, first, jnp.where(kind < 12, x, y))
            high = value.astype(jnp.bfloat16).astype(jnp.float32)
            rest = value - high
            middle = rest.astype(jnp.bfloat16).astype(jnp.float32)
            low = rest - middle
            total = (
                high * table_ref[base] + middle * table_ref[base + 1]
                + low * table_ref[base + 2] + table_ref[base + 3]
            )
            return total.astype(jnp.bfloat16)

        a_ref[r * cols_all + c] = parts(own, 0)
        b_ref[r * cols_all + c] = parts(near, 4)

    loop_cells(0, rows_all, 0, cols_all, factors, 8)

    def density(keep, r, c):
        acc = jnp.zeros((slots, slots), jnp.float32)
        left = a_ref[r * cols_all + c]
        cell = (r - 2) * span + (c - 2)
        for k, (sx, sy) in enumerate(STEPS):
            f = lax.dot_general(
                left, b_ref[(r + sx) * cols_all + c + sy], (((0,), (0,)), ((), ())),
                preferred_element_type=jnp.float32,
            )
            f = jnp.maximum(f, 0.0)
            square = f * f
            if keep:
                w_ref[cell, k] = square
            acc = acc + square * (f * field(2, r + sx, c + sy))
        value = 1.0 + jnp.sum(acc.T, axis=0, keepdims=True)
        full_ref[r, pl.ds(c, 1), :] = value
        inv_ref[r, pl.ds(c, 1), :] = value * (1.0 / (2.0 * PAIR_SCALE))

    kept, edge = functools.partial(density, True), functools.partial(density, False)
    loop_cells(2, rows_all - 2, 2, cols_all - 2, kept)
    for r in (1, rows_all - 2):
        loop_cells(r, r + 1, 1, cols_all - 1, edge)
    for c in (1, cols_all - 2):
        loop_cells(2, rows_all - 2, c, c + 1, edge)

    def weights(r, c):
        r0, c0 = r - 2, c - 2
        cell = r0 * span + c0
        dc = column(inv_ref[r, pl.ds(c, 1), :])
        acc = jnp.zeros((slots, slots), jnp.float32)
        for k, (sx, sy) in enumerate(STEPS):
            near = inv_ref[r + sx, pl.ds(c + sy, 1), :]
            weight = w_ref[cell, k] * pl.reciprocal(dc + near)
            w_ref[cell, k] = weight
            acc = acc + weight
        occupied = jnp.where(field(2, r, c) > 0.0, 1.0, 0.0)
        diagonal = BASE_STIFF + occupied * jnp.sum(acc.T, axis=0, keepdims=True)
        aux_ref[0, r0, pl.ds(c0, 1), :] = diagonal
        aux_ref[1, r0, pl.ds(c0, 1), :] = occupied / diagonal
        u_ref[r0, pl.ds(c0, 1), :] = field(3, r, c) / diagonal

    loop_cells(2, rows_all - 2, 2, cols_all - 2, weights)
    dens_ref[...] = full_ref[halo:halo + rows, halo:halo + cols, :]


def product(w_ref, aux_ref, u_ref, out_ref, reach, shift):
    rows, cols, slots = out_ref.shape
    skip = DEPTH - reach
    span = aux_ref.shape[2]

    def visit(r, c):
        cell = (r + skip) * span + (c + skip)
        acc = jnp.zeros((slots, slots), jnp.float32)
        for k, (sx, sy) in enumerate(STEPS):
            acc = acc + w_ref[cell, k] * u_ref[r + 1 + sx, pl.ds(c + 1 + sy, 1), :]
        summed = jnp.sum(acc.T, axis=0, keepdims=True)
        own = u_ref[r + 1, pl.ds(c + 1, 1), :]
        out_ref[r, pl.ds(c, 1), :] = (
            (1.0 - shift) * own - summed * aux_ref[1, r + skip, pl.ds(c + skip, 1), :]
        ) * (1.0 / SCALE)

    loop_cells(0, rows, 0, cols, visit, 5)


def own_part(ref, rows, cols):
    edge = (ref.shape[-3] - rows) // 2
    if edge == 0:
        return ref[...]
    return ref[..., edge:edge + rows, edge:edge + cols, :]


def products_kernel(first, count, last, *refs):
    w_ref, aux_ref, u_ref = refs[:3]
    earlier = refs[3:3 + (first + 1 if last else 0)]
    tail = refs[3 + len(earlier):]
    outs = tail[:count]
    grids = tail[count + (1 if last else 0):]
    rows, cols, slots = outs[0].shape
    source = u_ref
    for n in range(count):
        reach = count - 1 - n
        target = outs[n] if reach == 0 else grids[n]
        product(w_ref, aux_ref, source, target, reach, SHIFTS[first + n])
        if reach:
            outs[n][...] = own_part(target, rows, cols)
        source = target
    if last:
        gram_ref = tail[count]
        diagonal = own_part(aux_ref, rows, cols)[0]
        basis = [own_part(r, rows, cols) for r in earlier] + [r[...] for r in outs]
        lines = []
        for i, j in GRAM:
            term = basis[i] * basis[j] * diagonal
            lines.append(jnp.sum(jnp.sum(term, axis=0), axis=0, keepdims=True))
        lines += [jnp.zeros((1, slots), jnp.float32)] * (GRAM_ROWS - len(GRAM))
        gram_ref[...] = jnp.concatenate(lines, axis=0)


def solve_kernel(gram_ref, aux_ref, *refs):
    basis_refs = refs[:ITERS + 1]
    pressure_ref, residual_ref, peak_ref = refs[ITERS + 1:]
    rows, cols, slots = pressure_ref.shape
    totals = jnp.sum(gram_ref[...], axis=1, keepdims=True)
    gram = {}
    for n, (i, j) in enumerate(GRAM):
        gram[i, j] = gram[j, i] = totals[n:n + 1, :]
    zero = jnp.zeros((1, 1), jnp.float32)

    def mapped(v):
        out = [None] * (len(v) + 1)
        for k in range(len(v) + 1):
            term = SHIFTS[k] * v[k] if k < len(v) else zero
            out[k] = term + (SCALE * v[k - 1] if k else zero)
        return out

    def inner(a, b):
        total = zero
        for i, ai in enumerate(a):
            line = zero
            for j, bj in enumerate(b):
                line = line + gram[i, j] * bj
            total = total + ai * line
        return total

    def added(a, b, scale):
        size = max(len(a), len(b))
        pad = lambda v: v + [zero] * (size - len(v))
        return [x + scale * y for x, y in zip(pad(a), pad(b))]

    diagonal = own_part(aux_ref, rows, cols)[0]
    basis = [own_part(r, rows, cols) for r in basis_refs]

    def expand(coefs):
        total = None
        for k, coef in enumerate(coefs):
            term = coef.reshape(1, 1, 1) * basis[k]
            total = term if total is None else total + term
        return total

    z = [jnp.ones((1, 1), jnp.float32)]
    p = list(z)
    x = []
    rz = inner(z, z)
    tops = []
    for step in range(ITERS):
        image = mapped(p)
        size = rz / inner(p, image)
        x = added(x, p, size)
        z = added(z, image, -size)
        residual = diagonal * expand(z)
        tops.append(jnp.max(jnp.max(jnp.abs(residual), axis=0), axis=0, keepdims=True))
        if step + 1 < ITERS:
            following = inner(z, z)
            p = added(z, p, following / rz)
            rz = following
    pressure_ref[...] = expand(x)
    residual_ref[...] = residual
    tops += [jnp.zeros((1, slots), jnp.float32)] * (8 - len(tops))
    peak = jnp.max(jnp.concatenate(tops, axis=0), axis=1, keepdims=True)
    peak_ref[...] = jnp.broadcast_to(peak, (8, slots))


def body(offsets, masses, counts, source):
    _, rows, cols, slots = offsets.shape
    f32 = jnp.float32
    live = jnp.arange(slots, dtype=jnp.int32)[None, None, :] < counts[:, :, None]
    fields = jnp.concatenate(
        [offsets, jnp.where(live, masses, 0.0)[None], jnp.where(live, source, 0.0)[None]]
    )
    padded = ghosted(fields, DEPTH + 2)
    cells = padded.shape[1] * padded.shape[2]
    span_r, span_c = rows + 2 * DEPTH, cols + 2 * DEPTH
    own = jax.ShapeDtypeStruct((rows, cols, slots), f32)
    density, weight, aux, vector = pl.pallas_call(
        setup_kernel,
        out_shape=(
            own,
            WEIGHT_SPACE((span_r * span_c, len(STEPS), slots, slots), f32),
            jax.ShapeDtypeStruct((2, span_r, span_c, slots), f32),
            jax.ShapeDtypeStruct((span_r, span_c, slots), f32),
        ),
        scratch_shapes=[
            pltpu.VMEM(padded.shape[1:], f32),
            pltpu.VMEM(padded.shape[1:], f32),
            pltpu.VMEM((cells, SPLIT_ROWS, slots), jnp.bfloat16),
            pltpu.VMEM((cells, SPLIT_ROWS, slots), jnp.bfloat16),
            pltpu.VMEM((8, SPLIT_ROWS, slots), f32),
        ],
        compiler_params=LIMIT,
        name="setup",
    )(padded)
    kept = weight
    basis = [vector]
    wide = vector
    reach = DEPTH
    while len(basis) <= ITERS:
        if reach == 0:
            reach = min(DEPTH + 1, ITERS + 1 - len(basis))
            wide = ghosted(basis[-1], reach)
        first = len(basis) - 1
        count = reach
        last = first + count == ITERS
        outs = [own] * count
        if last:
            outs.append(jax.ShapeDtypeStruct((GRAM_ROWS, slots), f32))
        grids = [
            pltpu.VMEM((rows + 2 * e, cols + 2 * e, slots), f32) for e in range(count - 1, 0, -1)
        ]
        got = pl.pallas_call(
            lambda *refs, a=first, n=count, z=last: products_kernel(a, n, z, *refs),
            out_shape=tuple(outs),
            scratch_shapes=grids,
            compiler_params=LIMIT,
            name=f"products_{first}",
        )(kept, aux, wide, *(basis if last else []))
        basis += list(got[:count])
        if last:
            gram = got[count]
        reach = 0
    gram = combined(gram, jnp.add)
    pressure, residual, peak = pl.pallas_call(
        solve_kernel,
        out_shape=(own, own, jax.ShapeDtypeStruct((8, slots), f32)),
        compiler_params=LIMIT,
        name="solve",
    )(gram, aux, *basis)
    peak = combined(peak, jnp.maximum)
    return density, pressure, residual, peak[:ITERS, 0]


WEIGHT_SPACE = jax.ShapeDtypeStruct


def solution(mesh):
    in_specs = (P(None, "gx", "gy", None), P("gx", "gy", None), P("gx", "gy"), P("gx", "gy", None))
    out_specs = (P("gx", "gy", None), P("gx", "gy", None), P("gx", "gy", None), P())
    return jax.shard_map(body, mesh=mesh, in_specs=in_specs, out_specs=out_specs, check_vma=False)
```

```python
import functools

import jax
import jax.numpy as jnp
from jax import lax
from jax.experimental import pallas as pl
from jax.experimental.pallas import tpu as pltpu
from jax.sharding import PartitionSpec as P

ITERS = 5
BASE_STIFF = 0.5
PAIR_SCALE = 0.05
STEPS = [(sx, sy) for sx in (-1, 0, 1) for sy in (-1, 0, 1)]
DEPTH = 1
SPLIT_ROWS = 32
DEAD = -1.0e6
SHIFTS = (1.0, 0.15, 0.55, 0.8, 0.3)
SCALE = 0.3
GRAM = [(i, j) for i in range(ITERS + 1) for j in range(i, ITERS + 1)]
GRAM_ROWS = -(-len(GRAM) // 8) * 8
LIMIT = pltpu.CompilerParams(vmem_limit_bytes=12 * 1024 * 1024)


def extended(block, axis, dim, width):
    count = lax.axis_size(axis)
    size = block.shape[dim]
    lows, highs = [], []
    hop, left = 1, width
    while left > 0:
        take = min(size, left)
        up = [(i, i + hop) for i in range(count - hop)]
        down = [(i + hop, i) for i in range(count - hop)]
        tail = lax.slice_in_dim(block, size - take, size, axis=dim)
        head = lax.slice_in_dim(block, 0, take, axis=dim)
        lows.insert(0, lax.ppermute(tail, axis, up))
        highs.append(lax.ppermute(head, axis, down))
        hop, left = hop + 1, left - take
    return jnp.concatenate(lows + [block] + highs, axis=dim)


def ghosted(block, width):
    rank = block.ndim
    return extended(extended(block, "gx", rank - 3, width), "gy", rank - 2, width)


def combined(part, combine):
    for axis in ("gx", "gy"):
        count = lax.axis_size(axis)
        window = 1
        while window < count:
            radix = next(k for k in (4, 2, 3, count // window) if (count // window) % k == 0)
            got = [part]
            for k in range(1, radix):
                group = radix * window
                pairs = [
                    (i, i // group * group + (i % group + k * window) % group)
                    for i in range(count)
                ]
                got.append(lax.ppermute(part, axis, pairs))
            part = got[0]
            for other in got[1:]:
                part = combine(part, other)
            window *= radix
    return part


def column(row):
    slots = row.shape[-1]
    return jnp.broadcast_to(row, (slots, slots)).T


def loop_cells(row_from, row_to, col_from, col_to, visit, most=2):
    count = col_to - col_from
    unroll = max(k for k in range(1, most + 1) if count % k == 0)

    def outer(r, carry):
        def inner(c, carry):
            visit(r, c)
            return carry
        return lax.fori_loop(col_from, col_to, inner, carry, unroll=unroll)
    lax.fori_loop(row_from, row_to, outer, 0)


def write_tables(table_ref, kind):
    pairs = ((0, 0), (0, 1), (1, 0), (1, 1), (0, 2), (2, 0))
    left = [(0, 1.0), (1, 1.0), (2, 1.0), (3, 1.0), (3, 1.0), (3, 1.0)]
    right = [(3, 1.0), (3, 1.0), (3, 1.0), (0, 1.0), (1, 1.0), (2, 1.0)]
    for _ in range(2):
        left += [(p, 2.0) for p, _ in pairs]
        right += [(q, 1.0) for _, q in pairs]
    for base, side in ((0, left), (4, right)):
        for part in range(4):
            value = jnp.zeros(kind.shape, jnp.float32)
            for row, (p, scale) in enumerate(side):
                if p == part:
                    value = jnp.where(kind == row, scale, value)
            table_ref[base + part] = value


def setup_kernel(f_ref, dens_ref, w_ref, aux_ref, u_ref, full_ref, inv_ref, a_ref, b_ref, table_ref):
    _, rows_all, cols_all, slots = f_ref.shape
    halo = DEPTH + 2
    rows, cols = rows_all - 2 * halo, cols_all - 2 * halo
    span = cols + 2 * DEPTH
    kind = lax.broadcasted_iota(jnp.int32, (SPLIT_ROWS, slots), 0)
    write_tables(table_ref, kind)

    def field(k, r, c):
        return f_ref[k, r, pl.ds(c, 1), :]

    def factors(r, c):
        x = field(0, r, c) + (jnp.float32(r) - 0.5 * rows_all)
        y = field(1, r, c) + (jnp.float32(c) - 0.5 * cols_all)
        own = 0.5 - (x * x + y * y)
        near = jnp.where(field(2, r, c) > 0.0, own, DEAD)
        x, y = (jnp.broadcast_to(v, kind.shape) for v in (x, y))

        def parts(first, base):
            value = jnp.where(kind < 6, first, jnp.where(kind < 12, x, y))
            high = value.astype(jnp.bfloat16).astype(jnp.float32)
            rest = value - high
            middle = rest.astype(jnp.bfloat16).astype(jnp.float32)
            low = rest - middle
            total = (
                high * table_ref[base] + middle * table_ref[base + 1]
                + low * table_ref[base + 2] + table_ref[base + 3]
            )
            return total.astype(jnp.bfloat16)

        a_ref[r * cols_all + c] = parts(own, 0)
        b_ref[r * cols_all + c] = parts(near, 4)

    loop_cells(0, rows_all, 0, cols_all, factors, 8)

    def density(keep, r, c):
        acc = jnp.zeros((slots, slots), jnp.float32)
        left = a_ref[r * cols_all + c]
        cell = (r - 2) * span + (c - 2)
        for k, (sx, sy) in enumerate(STEPS):
            f = lax.dot_general(
                left, b_ref[(r + sx) * cols_all + c + sy], (((0,), (0,)), ((), ())),
                preferred_element_type=jnp.float32,
            )
            f = jnp.maximum(f, 0.0)
            square = f * f
            if keep:
                w_ref[cell, k] = square
            acc = acc + square * (f * field(2, r + sx, c + sy))
        value = 1.0 + jnp.sum(acc.T, axis=0, keepdims=True)
        full_ref[r, pl.ds(c, 1), :] = value
        inv_ref[r, pl.ds(c, 1), :] = value * (1.0 / (2.0 * PAIR_SCALE))

    kept, edge = functools.partial(density, True), functools.partial(density, False)
    loop_cells(2, rows_all - 2, 2, cols_all - 2, kept)
    for r in (1, rows_all - 2):
        loop_cells(r, r + 1, 1, cols_all - 1, edge)
    for c in (1, cols_all - 2):
        loop_cells(2, rows_all - 2, c, c + 1, edge)

    def weights(r, c):
        r0, c0 = r - 2, c - 2
        cell = r0 * span + c0
        dc = column(inv_ref[r, pl.ds(c, 1), :])
        acc = jnp.zeros((slots, slots), jnp.float32)
        for k, (sx, sy) in enumerate(STEPS):
            near = inv_ref[r + sx, pl.ds(c + sy, 1), :]
            weight = w_ref[cell, k] * pl.reciprocal(dc + near)
            w_ref[cell, k] = weight
            acc = acc + weight
        occupied = jnp.where(field(2, r, c) > 0.0, 1.0, 0.0)
        diagonal = BASE_STIFF + occupied * jnp.sum(acc.T, axis=0, keepdims=True)
        aux_ref[0, r0, pl.ds(c0, 1), :] = diagonal
        aux_ref[1, r0, pl.ds(c0, 1), :] = occupied / diagonal
        u_ref[r0, pl.ds(c0, 1), :] = field(3, r, c) / diagonal

    loop_cells(2, rows_all - 2, 2, cols_all - 2, weights, 5)
    dens_ref[...] = full_ref[halo:halo + rows, halo:halo + cols, :]


def product(w_ref, aux_ref, u_ref, out_ref, reach, shift):
    rows, cols, slots = out_ref.shape
    skip = DEPTH - reach
    span = aux_ref.shape[2]

    def visit(r, c):
        cell = (r + skip) * span + (c + skip)
        acc = jnp.zeros((slots, slots), jnp.float32)
        for k, (sx, sy) in enumerate(STEPS):
            acc = acc + w_ref[cell, k] * u_ref[r + 1 + sx, pl.ds(c + 1 + sy, 1), :]
        summed = jnp.sum(acc.T, axis=0, keepdims=True)
        own = u_ref[r + 1, pl.ds(c + 1, 1), :]
        out_ref[r, pl.ds(c, 1), :] = (
            (1.0 - shift) * own - summed * aux_ref[1, r + skip, pl.ds(c + skip, 1), :]
        ) * (1.0 / SCALE)

    loop_cells(0, rows, 0, cols, visit, 5)


def own_part(ref, rows, cols):
    edge = (ref.shape[-3] - rows) // 2
    if edge == 0:
        return ref[...]
    return ref[..., edge:edge + rows, edge:edge + cols, :]


def products_kernel(first, count, last, *refs):
    w_ref, aux_ref, u_ref = refs[:3]
    earlier = refs[3:3 + (first + 1 if last else 0)]
    tail = refs[3 + len(earlier):]
    outs = tail[:count]
    grids = tail[count + (1 if last else 0):]
    rows, cols, slots = outs[0].shape
    source = u_ref
    for n in range(count):
        reach = count - 1 - n
        target = outs[n] if reach == 0 else grids[n]
        product(w_ref, aux_ref, source, target, reach, SHIFTS[first + n])
        if reach:
            outs[n][...] = own_part(target, rows, cols)
        source = target
    if last:
        gram_ref = tail[count]
        diagonal = own_part(aux_ref, rows, cols)[0]
        basis = [own_part(r, rows, cols) for r in earlier] + [r[...] for r in outs]
        lines = []
        for i, j in GRAM:
            term = basis[i] * basis[j] * diagonal
            lines.append(jnp.sum(jnp.sum(term, axis=0), axis=0, keepdims=True))
        lines += [jnp.zeros((1, slots), jnp.float32)] * (GRAM_ROWS - len(GRAM))
        gram_ref[...] = jnp.concatenate(lines, axis=0)


def solve_kernel(gram_ref, aux_ref, *refs):
    basis_refs = refs[:ITERS + 1]
    pressure_ref, residual_ref, peak_ref = refs[ITERS + 1:]
    rows, cols, slots = pressure_ref.shape
    totals = jnp.sum(gram_ref[...], axis=1, keepdims=True)
    gram = {}
    for n, (i, j) in enumerate(GRAM):
        gram[i, j] = gram[j, i] = totals[n:n + 1, :]
    zero = jnp.zeros((1, 1), jnp.float32)

    def mapped(v):
        out = [None] * (len(v) + 1)
        for k in range(len(v) + 1):
            term = SHIFTS[k] * v[k] if k < len(v) else zero
            out[k] = term + (SCALE * v[k - 1] if k else zero)
        return out

    def inner(a, b):
        total = zero
        for i, ai in enumerate(a):
            line = zero
            for j, bj in enumerate(b):
                line = line + gram[i, j] * bj
            total = total + ai * line
        return total

    def added(a, b, scale):
        size = max(len(a), len(b))
        pad = lambda v: v + [zero] * (size - len(v))
        return [x + scale * y for x, y in zip(pad(a), pad(b))]

    diagonal = own_part(aux_ref, rows, cols)[0]
    basis = [own_part(r, rows, cols) for r in basis_refs]

    def expand(coefs):
        total = None
        for k, coef in enumerate(coefs):
            term = coef.reshape(1, 1, 1) * basis[k]
            total = term if total is None else total + term
        return total

    z = [jnp.ones((1, 1), jnp.float32)]
    p = list(z)
    x = []
    rz = inner(z, z)
    tops = []
    for step in range(ITERS):
        image = mapped(p)
        size = rz / inner(p, image)
        x = added(x, p, size)
        z = added(z, image, -size)
        residual = diagonal * expand(z)
        tops.append(jnp.max(jnp.max(jnp.abs(residual), axis=0), axis=0, keepdims=True))
        if step + 1 < ITERS:
            following = inner(z, z)
            p = added(z, p, following / rz)
            rz = following
    pressure_ref[...] = expand(x)
    residual_ref[...] = residual
    tops += [jnp.zeros((1, slots), jnp.float32)] * (8 - len(tops))
    peak = jnp.max(jnp.concatenate(tops, axis=0), axis=1, keepdims=True)
    peak_ref[...] = jnp.broadcast_to(peak, (8, slots))


def body(offsets, masses, counts, source):
    _, rows, cols, slots = offsets.shape
    f32 = jnp.float32
    live = jnp.arange(slots, dtype=jnp.int32)[None, None, :] < counts[:, :, None]
    fields = jnp.concatenate(
        [offsets, jnp.where(live, masses, 0.0)[None], jnp.where(live, source, 0.0)[None]]
    )
    padded = ghosted(fields, DEPTH + 2)
    cells = padded.shape[1] * padded.shape[2]
    span_r, span_c = rows + 2 * DEPTH, cols + 2 * DEPTH
    own = jax.ShapeDtypeStruct((rows, cols, slots), f32)
    density, weight, aux, vector = pl.pallas_call(
        setup_kernel,
        out_shape=(
            own,
            WEIGHT_SPACE((span_r * span_c, len(STEPS), slots, slots), f32),
            jax.ShapeDtypeStruct((2, span_r, span_c, slots), f32),
            jax.ShapeDtypeStruct((span_r, span_c, slots), f32),
        ),
        scratch_shapes=[
            pltpu.VMEM(padded.shape[1:], f32),
            pltpu.VMEM(padded.shape[1:], f32),
            pltpu.VMEM((cells, SPLIT_ROWS, slots), jnp.bfloat16),
            pltpu.VMEM((cells, SPLIT_ROWS, slots), jnp.bfloat16),
            pltpu.VMEM((8, SPLIT_ROWS, slots), f32),
        ],
        compiler_params=LIMIT,
        name="setup",
    )(padded)
    kept = weight
    basis = [vector]
    wide = vector
    reach = DEPTH
    while len(basis) <= ITERS:
        if reach == 0:
            reach = min(DEPTH + 1, ITERS + 1 - len(basis))
            wide = ghosted(basis[-1], reach)
        first = len(basis) - 1
        count = reach
        last = first + count == ITERS
        outs = [own] * count
        if last:
            outs.append(jax.ShapeDtypeStruct((GRAM_ROWS, slots), f32))
        grids = [
            pltpu.VMEM((rows + 2 * e, cols + 2 * e, slots), f32) for e in range(count - 1, 0, -1)
        ]
        got = pl.pallas_call(
            lambda *refs, a=first, n=count, z=last: products_kernel(a, n, z, *refs),
            out_shape=tuple(outs),
            scratch_shapes=grids,
            compiler_params=LIMIT,
            name=f"products_{first}",
        )(kept, aux, wide, *(basis if last else []))
        basis += list(got[:count])
        if last:
            gram = got[count]
        reach = 0
    gram = combined(gram, jnp.add)
    pressure, residual, peak = pl.pallas_call(
        solve_kernel,
        out_shape=(own, own, jax.ShapeDtypeStruct((8, slots), f32)),
        compiler_params=LIMIT,
        name="solve",
    )(gram, aux, *basis)
    peak = combined(peak, jnp.maximum)
    return density, pressure, residual, peak[:ITERS, 0]


WEIGHT_SPACE = jax.ShapeDtypeStruct


def solution(mesh):
    in_specs = (P(None, "gx", "gy", None), P("gx", "gy", None), P("gx", "gy"), P("gx", "gy", None))
    out_specs = (P("gx", "gy", None), P("gx", "gy", None), P("gx", "gy", None), P())
    return jax.shard_map(body, mesh=mesh, in_specs=in_specs, out_specs=out_specs, check_vma=False)
```
